256 devices in a mesh: dp: 16 (over z_hi, y, core), tensor: 16 (over z_lo, x).
Axes of the slice: x: 4, y: 4, z: 8 (z_hi: 2, z_lo: 4; z = z_hi * 4 + z_lo), core: 2. Of those that a mesh axis runs over, the one named last changes fastest.
Arguments:
- inputs: bfloat16 [4096, 8192], P('dp', 'tensor'), may hold values from -6 to 6
- gate_pre: bfloat16 [4096, 28672], P('dp', 'tensor'), may hold values from -6 to 6
- up_out: bfloat16 [4096, 28672], P('dp', 'tensor'), may hold values from -6 to 6
- down_weight: bfloat16 [28672, 8192], P('tensor', 'dp'), may hold values from -0.0625 to 0.0625
- out_grad: bfloat16 [4096, 8192], P('dp'), may hold values from -6 to 6
- seed_in: int32 [8192, 64], P('tensor'), may hold values from -2 to 2
- seed_out: int32 [28672, 64], P('tensor'), may hold values from -2 to 2
- queries: bfloat16 [65536, 4096], P(('dp', 'tensor')), may hold values from -0.09375 to 0.09375
Outputs:
- grads: float32 [16, 4096], P('dp')
- scores: float32 [16, 65536], P(None, ('dp', 'tensor'))
The draws below stay inside these ranges and needn't reach their ends.
All inputs are finite; a program needn't handle non-finite values.
Results may differ from the reference program's by a relative error of at most 0.01.
Values may be sent and summed in bfloat16 or wider, within the bound.
No kernel may reach another device: no remote copies, remote signals or barrier semaphores. Data moves between devices by JAX's collectives and lax.ppermute only.
A program may use at most 128 MiB of HBM per device.

```python
import jax
import jax.numpy as jnp
from jax import lax

D = 8192
FF = 28672
RANK = 64
SEQ_LEN = 256
EXAMPLES = 16
TOKENS = 4096
QUERIES = 65536
GDIM = 4096
N_DP = 16


def set_ends(drawn, rng, smallest, largest):
    dims = drawn.shape
    place = [jax.random.randint(jax.random.fold_in(rng, axis), (), 0, dims[axis]) for axis in range(len(dims))]
    drawn = drawn.at[tuple(place)].set(smallest)
    longest = dims.index(max(dims))
    place[longest] = (place[longest] + 1) % dims[longest]
    return drawn.at[tuple(place)].set(largest)


def shard_levels(key, dims, split, low, high):
    def one(dim, parts):
        heights = jax.random.uniform(jax.random.fold_in(jax.random.fold_in(key, 6), dim), (parts,), jnp.float32, low / len(split), high / len(split))
        return jnp.repeat(jnp.exp(heights), dims[dim] // parts).reshape((-1,) + (1,) * (len(dims) - dim - 1))

    level = one(*split[0])
    for cut in split[1:]:
        level = level * one(*cut)
    return level


def normal_values(own_key, extent, scale, bound, shards=(), dtype=jnp.bfloat16):
    drawn = scale * jax.random.normal(own_key, extent, jnp.float32)
    if shards:
        drawn = drawn * shard_levels(own_key, extent, shards, -0.22, 0.18)
    return jnp.clip(drawn, -bound, bound).astype(dtype)


def setup_inputs(seed: int = 0) -> dict:
    key_list = jax.random.split(jax.random.key(seed), 9)
    inputs = normal_values(key_list[0], (TOKENS, D), 1.0, 6.0, ((0, 16), (1, 16)))
    gate_pre = normal_values(key_list[1], (TOKENS, FF), 1.5, 6.0, ((0, 16), (1, 16)))
    up_out = normal_values(key_list[2], (TOKENS, FF), 1.0, 6.0, ((0, 16), (1, 16)))
    down_weight = normal_values(key_list[3], (FF, D), D ** -0.5, 0.0625, ((0, 16), (1, 16)))
    out_grad = normal_values(key_list[4], (TOKENS, D), 1.0, 6.0, ((0, 16),))
    seed_in = set_ends(jax.random.randint(key_list[5], (D, RANK), -2, 3), jax.random.fold_in(key_list[5], 1), -2, 2).astype(jnp.int32)
    seed_out = set_ends(jax.random.randint(key_list[6], (FF, RANK), -2, 3), jax.random.fold_in(key_list[6], 1), -2, 2).astype(jnp.int32)
    queries = normal_values(key_list[7], (QUERIES, GDIM), GDIM ** -0.5, 0.09375, ((0, 256),))
    return dict(inputs=inputs, gate_pre=gate_pre, up_out=up_out, down_weight=down_weight, out_grad=out_grad, seed_in=seed_in, seed_out=seed_out, queries=queries)


def reference(inputs, gate_pre, up_out, down_weight, out_grad, seed_in, seed_out, queries):
    block = D // N_DP
    hidden_grad = jnp.zeros((TOKENS, FF), jnp.float32)
    for index in range(N_DP):
        cols = out_grad[:, index * block:(index + 1) * block]
        wcols = down_weight[:, index * block:(index + 1) * block]
        partial_term = lax.dot_general(cols, wcols, (((1,), (1,)), ((), ())), preferred_element_type=jnp.float32)
        rounded = lax.optimization_barrier(partial_term.astype(jnp.bfloat16))
        hidden_grad = hidden_grad + rounded.astype(jnp.float32)
    gate_f = gate_pre.astype(jnp.float32)
    sigma = jax.nn.sigmoid(gate_f)
    gate_grad = (hidden_grad * up_out.astype(jnp.float32) * sigma * (1.0 + gate_f * (1.0 - sigma))).astype(jnp.bfloat16)
    proj_in = (seed_in.astype(jnp.float32) * (2.0 * D) ** -0.5).astype(jnp.bfloat16)
    proj_out = (seed_out.astype(jnp.float32) * 0.25 * (2.0 * FF) ** -0.5).astype(jnp.bfloat16)
    left = jnp.dot(inputs, proj_in, preferred_element_type=jnp.float32)
    right = jnp.dot(gate_grad, proj_out, preferred_element_type=jnp.float32)
    left = left.reshape(EXAMPLES, SEQ_LEN, RANK)
    right = right.reshape(EXAMPLES, SEQ_LEN, RANK)
    grads = jnp.einsum("esr,esc->erc", left, right).reshape(EXAMPLES, GDIM)
    scores = lax.dot_general(grads.astype(jnp.bfloat16), queries, (((1,), (1,)), ((), ())), preferred_element_type=jnp.float32)
    return grads, scores
```

```python
import jax
import jax.numpy as jnp
from jax import lax
from jax.sharding import Mesh, PartitionSpec as P

D = 8192
FF = 28672
BF = jnp.bfloat16
F32 = jnp.float32
DP = ("zh", "y", "c")
TP = ("zl", "x")


def flip(v, axis):
    return lax.ppermute(v, axis, [(0, 1), (1, 0)])


def fetch(v, axis, step):
    return lax.ppermute(v, axis, [((i + step) % 4, i) for i in range(4)])


def everyone(v, axes, count):
    copies = jnp.broadcast_to(v[None], (count,) + v.shape)
    return lax.all_to_all(copies, axes, 0, 0, tiled=True)


def mul_t(rows, weight):
    return lax.dot_general(rows, weight, (((1,), (1,)), ((), ())), preferred_element_type=F32)


def after(value, *first):
    return lax.optimization_barrier((value,) + first)[0]


def on_device(inputs, gate_pre, up_out, weight, out_grad, seed_in, seed_out, queries):
    seq, block = out_grad.shape[0], weight.shape[1]
    ff = weight.shape[0]
    half = ff // 2
    rank = seed_in.shape[1]
    zh, y, c, x = (lax.axis_index(name) for name in ("zh", "y", "c", "x"))

    def columns(z, s, core, width=block):
        return lax.dynamic_slice(out_grad, (0, (z * 8 + s * 2 + core) * block), (seq, width))

    w_prev = fetch(weight, "y", 3)
    w_next = fetch(weight, "y", 1)
    z_rows = flip(columns(1 - zh, (y + x) % 4, 0, 2 * block), "zh")
    own_cols = jnp.concatenate([columns(zh, (y + j) % 4, c) for j in range(4)], axis=1)
    mate_cols = flip(
        jnp.concatenate([columns(zh, (y + j) % 4, 1 - c) for j in range(4)], axis=1), "c"
    )

    gate = gate_pre.astype(F32)
    sigma = jax.nn.sigmoid(gate)
    act = (up_out.astype(F32) * sigma * (1.0 + gate * (1.0 - sigma))).astype(BF)
    act_z = flip(after(act, z_rows), "zh") if False else flip(act, "zh")
    act_c = flip(act, "c")

    proj_in = (seed_in.astype(F32) * (2.0 * D) ** (-0.5)).astype(BF)
    proj_out = (seed_out.astype(F32) * 0.25 * (2.0 * FF) ** (-0.5)).astype(BF)
    left = jnp.dot(inputs, proj_in, preferred_element_type=F32).astype(BF)
    left = sum(fetch(left, "x", s).astype(F32) for s in (1, 2, 3)) + left.astype(F32)
    left_all = everyone(left.astype(BF), ("zh", "zl"), 8).reshape(2, 4, seq, rank)
    left_all = left_all.astype(F32).sum(1)
    left_own = lax.dynamic_index_in_dim(left_all, zh, 0, False)
    left_far = lax.dynamic_index_in_dim(left_all, 1 - zh, 0, False)
    left_pair = jnp.stack([left_own, left_far]).astype(BF)
    left_mate = flip(left_pair, "c")
    lefts = [left_pair[0], left_mate[0], left_pair[1], left_mate[1]]

    z_keep = lax.dynamic_slice(z_rows, (0, c * block), (seq, block))
    z_mate = flip(lax.dynamic_slice(z_rows, (0, (1 - c) * block), (seq, block)), "c")
    far = jnp.concatenate([z_keep, z_mate], axis=0)
    fars = jnp.stack([far] + [fetch(far, "x", s) for s in (1, 2, 3)])

    near_cols = jnp.concatenate([own_cols, mate_cols], axis=0)
    act_near = jnp.concatenate([act, act_c], axis=0)
    act_far = jnp.concatenate([act_z, flip(act_z, "c")], axis=0)

    w_opp = [fetch(w_prev[:half], "y", 3), fetch(w_next[half:], "y", 1)]

    def rows(j):
        far_j = lax.dynamic_index_in_dim(fars, (j - x) % 4, 0, False)
        return near_cols[:, j * block : (j + 1) * block], far_j

    right = [jnp.zeros((2 * seq, rank), F32)] * 2
    for h in range(2):
        span = slice(h * half, (h + 1) * half)
        slabs = (weight[span], w_next[span], w_opp[h], w_prev[span])
        for part, acts in enumerate((act_near, act_far)):
            hidden = sum(mul_t(rows(j)[part], slabs[j]) for j in (0, 1, 3, 2))
            grad = (hidden * acts[:, span].astype(F32)).astype(BF)
            right[part] = right[part] + jnp.dot(
                grad, proj_out[span], preferred_element_type=F32
            )
    rights = [right[0][:seq], right[0][seq:], right[1][:seq], right[1][seq:]]
    grads = jnp.stack(
        [
            lax.dot_general(l, r.astype(BF), (((0,), (0,)), ((), ())), preferred_element_type=F32)
            for l, r in zip(lefts, rights)
        ]
    ).reshape(4 * rank, rank)

    mine = grads.astype(BF)
    grads = grads + sum(fetch(mine, "x", s).astype(F32) for s in (1, 2, 3))
    z_all = everyone(grads.astype(BF), ("zh", "zl"), 8).reshape(2, 4, 4, rank, rank)
    z_all = z_all.astype(F32).sum(1)
    z_own = lax.dynamic_index_in_dim(z_all, zh, 0, False)
    z_far = lax.dynamic_index_in_dim(z_all, 1 - zh, 0, False)
    grads = z_own + jnp.concatenate([z_far[2:], z_far[:2]])
    mate = flip(grads.astype(BF), "c").astype(F32)
    grads = grads + jnp.stack([mate[1], mate[0], mate[3], mate[2]])
    every = everyone(grads.astype(BF).reshape(4, rank * rank), "y", 4).reshape(4, 2, 2, rank * rank)
    every = jnp.where(zh == 1, every[:, ::-1], every)
    every = jnp.where(c == 1, every[:, :, ::-1], every)
    every = every.transpose(1, 0, 2, 3).reshape(16, rank * rank)
    scores = mul_t(every, queries)
    return grads[0].reshape(1, rank * rank), scores


def solution(mesh):
    fine = Mesh(mesh.devices.reshape(2, 4, 2, 4, 4), DP + TP)
    in_specs = (
        P(DP, TP),
        P(DP, TP),
        P(DP, TP),
        P(TP, DP),
        P(DP, None),
        P(TP, None),
        P(TP, None),
        P(DP + TP, None),
    )
    out_specs = (P(DP, None), P(None, DP + TP))
    return jax.shard_map(
        on_device, mesh=fine, in_specs=in_specs, out_specs=out_specs, check_vma=False
    )
```

```python
import jax
import jax.numpy as jnp
from jax import lax
from jax.experimental import pallas as pl
from jax.experimental.pallas import tpu as pltpu
from jax.sharding import Mesh, PartitionSpec as P


D = 8192
FF = 28672
BF = jnp.bfloat16
F32 = jnp.float32
DP = ("zh", "y", "c")
TP = ("zl", "x")
WIDE = 896


def flip(v, axis):
    return lax.ppermute(v, axis, [(0, 1), (1, 0)])


def fetch(v, axis, step):
    return lax.ppermute(v, axis, [((i + step) % 4, i) for i in range(4)])


def everyone(v, axes, count):
    copies = jnp.broadcast_to(v[None], (count,) + v.shape)
    return lax.all_to_all(copies, axes, 0, 0, tiled=True)


def nt(rows, weight):
    return lax.dot_general(rows, weight, (((1,), (1,)), ((), ())), preferred_element_type=F32)


def spec_of(array, width, at):
    if array.ndim == 3:
        return pl.BlockSpec((None, array.shape[1], width), lambda i, s: (s[at], 0, s[at + 1]))
    return pl.BlockSpec((array.shape[0], width), lambda i, s: (0, s[at + 1]))


def near_sums(index, at, rows, mats, act, proj):
    n = len(mats)
    seq, ff = act.shape
    block, rank = mats[0].shape[1], proj.shape[1]

    def kernel(_, *refs):
        parts, mat = refs[:n], refs[n : 2 * n]
        act_ref, proj_ref, out = refs[2 * n :]

        @pl.when(pl.program_id(0) == 0)
        def _():
            out[...] = jnp.zeros_like(out)

        hidden = sum(nt(p[...], m[...]) for p, m in zip(parts, mat))
        grad = (hidden * act_ref[...].astype(F32)).astype(BF)
        out[...] += jnp.dot(grad, proj_ref[...], preferred_element_type=F32)

    return pl.pallas_call(
        kernel,
        out_shape=jax.ShapeDtypeStruct((seq, rank), F32),
        grid_spec=pltpu.PrefetchScalarGridSpec(
            num_scalar_prefetch=1,
            grid=(ff // WIDE,),
            in_specs=[spec_of(rows, block, at + 2 * t) for t in range(n)]
            + [pl.BlockSpec((WIDE, block), lambda i, s: (i, 0))] * n
            + [
                pl.BlockSpec((seq, WIDE), lambda i, s: (0, i)),
                pl.BlockSpec((WIDE, rank), lambda i, s: (i, 0)),
            ],
            out_specs=pl.BlockSpec((seq, rank), lambda i, s: (0, 0)),
        ),
    )(index, *([rows] * n), *mats, act, proj)


def far_sums(index, pieces, mats):
    n = len(mats)
    seq, ff = pieces[0].shape[0], mats[0].shape[0]
    block = mats[0].shape[1]

    def kernel(s, *refs):
        parts, mat = refs[:4], refs[4 : 4 + n]
        out, kept, rows, sems = refs[4 + n :]

        @pl.when(pl.program_id(0) == 0)
        def _():
            copies = [
                pltpu.make_async_copy(parts[r], rows.at[lax.rem(s[1] + r, 4)], sems.at[r])
                for r in range(4)
            ]
            for copy in copies:
                copy.start()
            for copy in copies:
                copy.wait()
            kept[...] = rows[2]

        total = None
        for t in range(n):
            at = pl.multiple_of(s[18 + 2 * t + 1] * block, block)
            term = nt(rows[s[18 + 2 * t], :, pl.ds(at, block)], mat[t][...])
            total = term if total is None else total + term
        out[...] = total

    return pl.pallas_call(
        kernel,
        out_shape=(
            jax.ShapeDtypeStruct((seq, ff), F32),
            jax.ShapeDtypeStruct((seq, 2 * block), BF),
        ),
        grid_spec=pltpu.PrefetchScalarGridSpec(
            num_scalar_prefetch=1,
            grid=(ff // WIDE,),
            in_specs=[pl.BlockSpec(memory_space=pl.ANY)] * 4
            + [pl.BlockSpec((WIDE, block), lambda i, s: (i, 0))] * n,
            out_specs=(
                pl.BlockSpec((seq, WIDE), lambda i, s: (0, i)),
                pl.BlockSpec((seq, 2 * block), lambda i, s: (0, 0)),
            ),
            scratch_shapes=[
                pltpu.VMEM((4, seq, 2 * block), BF),
                pltpu.SemaphoreType.DMA((4,)),
            ],
        ),
    )(index, *pieces, *mats)


def project(index, near_from, far_from, near, far, mats, right, sums, acts, proj, left_all):
    n = len(mats)
    seq, ff = sums.shape
    block, rank = mats[0].shape[1], proj.shape[1]
    half = rank // 2

    def kernel(s, *refs):
        near_parts, far_parts, mat = refs[:n], refs[n : 2 * n], refs[2 * n : 3 * n]
        right_ref, sum_ref, act_n, act_f, proj_ref, left_ref, out, right_n, right_f = refs[3 * n :]

        @pl.when(pl.program_id(0) == 0)
        def _():
            right_n[...] = right_ref[...]
            right_f[...] = jnp.zeros_like(right_f)

        hidden = sum(nt(p[...], m[...]) for p, m in zip(near_parts, mat))
        grad = (hidden * act_n[...].astype(F32)).astype(BF)
        right_n[...] += jnp.dot(grad, proj_ref[...], preferred_element_type=F32)
        hidden = sum_ref[...] + sum(nt(p[...], m[...]) for p, m in zip(far_parts, mat))
        grad = (hidden * act_f[...].astype(F32)).astype(BF)
        right_f[...] += jnp.dot(grad, proj_ref[...], preferred_element_type=F32)

        @pl.when(pl.program_id(0) == pl.num_programs(0) - 1)
        def _():
            zh = s[0]
            pieces = []
            for z, total in ((zh, right_n), (1 - zh, right_f)):
                left = sum(left_ref[4 * z + k].astype(F32) for k in range(4)).astype(BF)
                outer = jnp.dot(left, total[...].astype(BF), preferred_element_type=F32)
                pieces.append(jnp.concatenate([outer[:half], outer[half:]], axis=1).astype(BF))
            for copy in range(out.shape[0]):
                out[copy, :half, :] = pieces[0]
                out[copy, half:, :] = pieces[1]

    wide = pl.BlockSpec((seq, WIDE), lambda i, s: (0, i))
    return_shape = (8, rank, 2 * rank)
    return pl.pallas_call(
        kernel,
        out_shape=jax.ShapeDtypeStruct(return_shape, BF),
        grid_spec=pltpu.PrefetchScalarGridSpec(
            num_scalar_prefetch=1,
            grid=(ff // WIDE,),
            in_specs=[spec_of(near, block, near_from + 2 * t) for t in range(n)]
            + [spec_of(far, block, far_from + 2 * t) for t in range(n)]
            + [pl.BlockSpec((WIDE, block), lambda i, s: (i, 0))] * n
            + [pl.BlockSpec((seq, rank), lambda i, s: (0, 0)), wide, wide, wide]
            + [pl.BlockSpec((WIDE, rank), lambda i, s: (i, 0))]
            + [pl.BlockSpec(left_all.shape, lambda i, s: (0, 0, 0))],
            out_specs=pl.BlockSpec(return_shape, lambda i, s: (0, 0, 0)),
            scratch_shapes=[pltpu.VMEM((seq, rank), F32)] * 2,
        ),
    )(index, *([near] * n), *([far] * n), *mats, right, sums, *acts, proj, left_all)


def merge(parts):
    def kernel(ref, out):
        side = [
            [sum(ref[z, k, g].astype(F32) for k in range(4)) for g in range(2)] for z in range(2)
        ]
        first = (side[0][0] + side[1][1]).astype(BF)
        second = (side[1][0] + side[0][1]).astype(BF)
        for copy in range(out.shape[0]):
            out[copy, 0] = first
            out[copy, 1] = second

    return pl.pallas_call(
        kernel, out_shape=jax.ShapeDtypeStruct((32, 2) + parts.shape[3:], BF)
    )(parts)


def finish(me, parts, queries):
    rows, lanes = parts.shape[-2:]
    count = queries.shape[0]
    examples = parts.shape[0] * parts.shape[2] * parts.shape[3]

    def kernel(me_ref, ref, q_ref, grads_ref, scores_ref, table):
        for y in range(4):
            for core in range(2):
                for z in range(2):
                    e = z * 8 + y * 2 + core
                    table[e * rows : (e + 1) * rows, :] = sum(
                        ref[y, k, core, z].astype(F32) for k in range(4)
                    )
        total = jnp.zeros((examples, count), F32)
        for k in range(rows):
            span = slice(k * lanes, (k + 1) * lanes)
            piece = table[pl.ds(k, examples, stride=rows), :].astype(BF)
            total = total + nt(piece, q_ref[:, span])
            grads_ref[:, span] = table[pl.ds(me_ref[0] * rows + k, 1), :]
        scores_ref[...] = total

    return pl.pallas_call(
        kernel,
        out_shape=(
            jax.ShapeDtypeStruct((1, rows * lanes), F32),
            jax.ShapeDtypeStruct((examples, count), F32),
        ),
        in_specs=[
            pl.BlockSpec(memory_space=pltpu.SMEM),
            pl.BlockSpec(memory_space=pltpu.VMEM),
            pl.BlockSpec(memory_space=pltpu.VMEM),
        ],
        out_specs=(pl.BlockSpec(memory_space=pltpu.VMEM), pl.BlockSpec(memory_space=pltpu.VMEM)),
        scratch_shapes=[pltpu.VMEM((examples * rows, lanes), F32)],
    )(me, parts, queries)


def along_y(v, forward):
    pairs = []
    for y in range(4):
        for core in range(2):
            step = 1 if (core == 0) == forward else 3
            pairs.append((2 * y + core, 2 * ((y + step) % 4) + core))
    return lax.ppermute(v, ("y", "c"), pairs)


def trade(copies, axes):
    return lax.all_to_all(copies, axes, 0, 0, tiled=True)


def on_device(inputs, gate_pre, up_out, weight, out_grad, seed_in, seed_out, queries):
    seq, block = out_grad.shape[0], weight.shape[1]
    rank = seed_in.shape[1]
    zh, y, c, x = (lax.axis_index(name).astype(jnp.int32) for name in ("zh", "y", "c", "x"))

    w_one = along_y(weight, True)
    w_two = along_y(weight, False)
    m_own = flip(weight, "c")
    start = ((1 - zh) * 8 + ((y + x) % 4) * 2) * block
    far = flip(lax.dynamic_slice(out_grad, (0, start), (seq, 2 * block)), "zh")

    proj = (seed_out.astype(F32) * 0.25 * (2.0 * FF) ** (-0.5)).astype(BF)
    gate = gate_pre.astype(F32)
    sigma = jax.nn.sigmoid(gate)
    act = (up_out.astype(F32) * sigma * (1.0 + gate * (1.0 - sigma))).astype(BF)
    one, two = jnp.where(c == 0, 3, 1), jnp.where(c == 0, 1, 3)
    slabs = [(0, c), (0, 1 - c), (one, c), (two, 1 - c), (two, c), (one, 1 - c), (2, c), (2, 1 - c)]
    index = [zh, x]
    for j, core in slabs:
        index += [zh, zh * 8 + ((y + j) % 4) * 2 + core]
    for j, core in slabs:
        index += [jnp.int32(j), core]
    index = jnp.stack([jnp.asarray(v, jnp.int32) for v in index])
    act, proj, index = lax.optimization_barrier((act, proj, index))
    act_far = flip(act, "zh")

    order = jnp.concatenate([jnp.arange(0, rank, 2), jnp.arange(1, rank, 2)])
    pick = (jnp.arange(rank)[:, None] == order[None, :]).astype(BF)
    proj_in = (seed_in.astype(F32) * (2.0 * D) ** (-0.5)).astype(BF)
    proj_in = jnp.dot(proj_in, pick, preferred_element_type=F32).astype(BF)
    left = lax.dot_general(
        proj_in, inputs, (((0,), (1,)), ((), ())), preferred_element_type=F32
    ).astype(BF)
    left = sum(fetch(left, "x", s).astype(F32) for s in (1, 2, 3)) + left.astype(F32)
    left_all = everyone(left.astype(BF), ("zh", "zl"), 8)

    fars = [far] + [fetch(far, "x", s) for s in (1, 2, 3)]

    m_one = flip(w_one, "c")
    m_two = flip(w_two, "c")
    w_opp = along_y(w_one, True)
    m_opp = flip(w_opp, "c")

    mats = (weight, m_own, w_one, m_one, w_two, m_two)
    right = near_sums(index, 2, out_grad, mats, act, proj)
    sum_far, far_opp = far_sums(index, fars, mats)
    payload = project(
        index, 14, 30, out_grad, far_opp, (w_opp, m_opp), right, sum_far, (act, act_far), proj,
        left_all,
    )
    z_all = trade(payload, ("zh", "zl"))
    merged = merge(z_all.reshape(2, 4, 2, rank // 2, 2 * rank))
    every = trade(merged, ("y", "x", "c"))
    me = (zh * 8 + y * 2 + c).reshape(1)
    every = every.reshape(4, 4, 2, 2, rank // 2, 2 * rank)
    return finish(me, every, queries)


def solution(mesh):
    fine = Mesh(mesh.devices.reshape(2, 4, 2, 4, 4), DP + TP)
    in_specs = (
        P(DP, TP),
        P(DP, TP),
        P(DP, TP),
        P(TP, DP),
        P(DP, None),
        P(TP, None),
        P(TP, None),
        P(DP + TP, None),
    )
    out_specs = (P(DP, None), P(None, DP + TP))

    return jax.shard_map(
        on_device, mesh=fine, in_specs=in_specs, out_specs=out_specs, check_vma=False
    )
```

```python
import jax
import jax.numpy as jnp
from jax import lax
from jax.experimental import pallas as pl
from jax.experimental.pallas import tpu as pltpu
from jax.sharding import Mesh, PartitionSpec as P


D = 8192
FF = 28672
BF = jnp.bfloat16
F32 = jnp.float32
DP = ("zh", "y", "c")
TP = ("zl", "x")
WIDE = 896
TILE = 256


def flip(v, axis):
    return lax.ppermute(v, axis, [(0, 1), (1, 0)])


def fetch(v, axis, step):
    return lax.ppermute(v, axis, [((i + step) % 4, i) for i in range(4)])


def everyone(v, axes, count):
    copies = jnp.broadcast_to(v[None], (count,) + v.shape)
    return lax.all_to_all(copies, axes, 0, 0, tiled=True)


def nt(rows, weight):
    return lax.dot_general(rows, weight, (((1,), (1,)), ((), ())), preferred_element_type=F32)


def slab_sums(index, near, pieces_a, pieces_b, mats, act, proj):
    n = len(mats)
    seq, ff = act.shape
    block, rank = mats[0].shape[1], proj.shape[1]
    half, pair = seq // 2, 2 * block

    def kernel(s, *refs):
        near_ref, parts_a, parts_b, mat = refs[0], refs[1:5], refs[5:9], refs[9 : 9 + n]
        act_ref, proj_ref, right, out, kept, rows, sems = refs[9 + n :]

        @pl.when(pl.program_id(0) == 0)
        def _():
            copies = []
            for j in range(4):
                at = pl.multiple_of(s[4 + j] * block, block)
                source = near_ref.at[:, pl.ds(at, pair)]
                copies.append((source, rows.at[j, pl.ds(0, seq)]))
            for r in range(4):
                slot = lax.rem(s[1] + r, 4)
                at_a = pl.multiple_of(seq + s[2] * half, half)
                at_b = pl.multiple_of(seq + (1 - s[2]) * half, half)
                copies.append((parts_a[r], rows.at[slot, pl.ds(at_a, half)]))
                copies.append((parts_b[r], rows.at[slot, pl.ds(at_b, half)]))
            copies = [
                pltpu.make_async_copy(source, target, sems.at[k])
                for k, (source, target) in enumerate(copies)
            ]
            for copy in copies:
                copy.start()
            for copy in copies:
                copy.wait()
            kept[...] = rows[2]
            right[...] = jnp.zeros_like(right)

        total = None
        for t in range(n):
            at = pl.multiple_of(s[8 + 2 * t + 1] * block, block)
            term = nt(rows[s[8 + 2 * t], :, pl.ds(at, block)], mat[t][...])
            total = term if total is None else total + term
        out[...] = total[seq:]
        grad = (total[:seq] * act_ref[...].astype(F32)).astype(BF)
        right[...] += jnp.dot(grad, proj_ref[...], preferred_element_type=F32)

    return pl.pallas_call(
        kernel,
        out_shape=(
            jax.ShapeDtypeStruct((seq, rank), F32),
            jax.ShapeDtypeStruct((seq, ff), F32),
            jax.ShapeDtypeStruct((2 * seq, pair), BF),
        ),
        grid_spec=pltpu.PrefetchScalarGridSpec(
            num_scalar_prefetch=1,
            grid=(ff // TILE,),
            in_specs=[pl.BlockSpec(memory_space=pl.ANY)] * 9
            + [pl.BlockSpec((TILE, block), lambda i, s: (i, 0))] * n
            + [
                pl.BlockSpec((seq, TILE), lambda i, s: (0, i)),
                pl.BlockSpec((TILE, rank), lambda i, s: (i, 0)),
            ],
            out_specs=(
                pl.BlockSpec((seq, rank), lambda i, s: (0, 0)),
                pl.BlockSpec((seq, TILE), lambda i, s: (0, i)),
                pl.BlockSpec((2 * seq, pair), lambda i, s: (0, 0)),
            ),
            scratch_shapes=[
                pltpu.VMEM((4, 2 * seq, pair), BF),
                pltpu.SemaphoreType.DMA((12,)),
            ],
        ),
    )(index, near, *pieces_a, *pieces_b, *mats, act, proj)


def middle(index, rows, mat, right, sums, act, proj):
    seq, ff = sums.shape
    block, rank = mat.shape[1], proj.shape[1]

    def kernel(_, rows_ref, mat_ref, right_ref, sum_ref, act_ref, proj_ref, out, sum_out):
        @pl.when(pl.program_id(0) == 0)
        def _():
            out[...] = right_ref[...]

        total = nt(rows_ref[...], mat_ref[...])
        sum_out[...] = sum_ref[...] + total[seq:]
        grad = (total[:seq] * act_ref[...].astype(F32)).astype(BF)
        out[...] += jnp.dot(grad, proj_ref[...], preferred_element_type=F32)

    wide = pl.BlockSpec((seq, WIDE), lambda i, s: (0, i))
    small = pl.BlockSpec((seq, rank), lambda i, s: (0, 0))
    return pl.pallas_call(
        kernel,
        out_shape=(jax.ShapeDtypeStruct((seq, rank), F32), jax.ShapeDtypeStruct((seq, ff), F32)),
        grid_spec=pltpu.PrefetchScalarGridSpec(
            num_scalar_prefetch=1,
            grid=(ff // WIDE,),
            in_specs=[
                pl.BlockSpec((2 * seq, block), lambda i, s: (0, s[21])),
                pl.BlockSpec((WIDE, block), lambda i, s: (i, 0)),
                small,
                wide,
                wide,
                pl.BlockSpec((WIDE, rank), lambda i, s: (i, 0)),
            ],
            out_specs=(small, wide),
        ),
    )(index, rows, mat, right, sums, act, proj)


def project(index, rows, mat, right, sums, acts, proj, left_all):
    seq, ff = sums.shape
    block, rank = mat.shape[1], proj.shape[1]
    half = rank // 2
    steps = ff // WIDE

    def kernel(s, rows_hbm, mat_ref, right_hbm, sum_hbm, near_hbm, act_f, proj_hbm, left_ref,
               out, rows_ref, right_n, sum_ref, act_n, proj_ref, sems):
        at = pl.multiple_of(s[23] * block, block)
        moves = [(rows_hbm.at[:, pl.ds(at, block)], rows_ref)]
        waits = []
        for k in range(steps):
            span = pl.ds(k * WIDE, WIDE)
            waits.append(len(moves))
            moves += [
                (near_hbm.at[:, span], act_n.at[:, span]),
                (proj_hbm.at[span], proj_ref.at[span]),
                (sum_hbm.at[:, span], sum_ref.at[:, span]),
            ]
            if k == 0:
                moves.append((right_hbm, right_n))
        waits.append(len(moves))
        copies = [
            pltpu.make_async_copy(source, target, sems.at[k])
            for k, (source, target) in enumerate(moves)
        ]
        for copy in copies:
            copy.start()
        copies[0].wait()
        sides = [None, None]
        for k in range(steps):
            for copy in copies[waits[k] : waits[k + 1]]:
                copy.wait()
            span = slice(k * WIDE, (k + 1) * WIDE)
            total = nt(rows_ref[...], mat_ref[span, :])
            hiddens = (total[:seq], sum_ref[:, span] + total[seq:])
            for i, (hidden, act) in enumerate(zip(hiddens, (act_n, act_f))):
                grad = (hidden * act[:, span].astype(F32)).astype(BF)
                term = jnp.dot(grad, proj_ref[span, :], preferred_element_type=F32)
                sides[i] = term if sides[i] is None else sides[i] + term
        sides[0] = sides[0] + right_n[...]
        pieces = []
        for z, side in ((s[0], sides[0]), (1 - s[0], sides[1])):
            left = sum(left_ref[4 * z + k].astype(F32) for k in range(4)).astype(BF)
            outer = jnp.dot(left, side.astype(BF), preferred_element_type=F32)
            pieces.append(jnp.concatenate([outer[:half], outer[half:]], axis=1).astype(BF))
        for copy in range(out.shape[0]):
            out[copy, :half, :] = pieces[0]
            out[copy, half:, :] = pieces[1]

    hbm = pl.BlockSpec(memory_space=pltpu.HBM)
    vmem = pl.BlockSpec(memory_space=pltpu.VMEM)
    mat, act_far, left_all = (
        pltpu.with_memory_space_constraint(v, pltpu.VMEM) for v in (mat, acts[1], left_all)
    )
    return pl.pallas_call(
        kernel,
        out_shape=jax.ShapeDtypeStruct((8, rank, 2 * rank), BF),
        in_specs=[pl.BlockSpec(memory_space=pltpu.SMEM), hbm, vmem, hbm, hbm, hbm, vmem, hbm, vmem],
        out_specs=vmem,
        scratch_shapes=[
            pltpu.VMEM((2 * seq, block), BF),
            pltpu.VMEM(right.shape, F32),
            pltpu.VMEM(sums.shape, F32),
            pltpu.VMEM(sums.shape, BF),
            pltpu.VMEM(proj.shape, BF),
            pltpu.SemaphoreType.DMA((2 + 3 * steps,)),
        ],
    )(index, rows, mat, right, sums, acts[0], act_far, proj, left_all)


def merge(parts):
    def kernel(ref, out):
        side = [
            [sum(ref[z, k, g].astype(F32) for k in range(4)) for g in range(2)] for z in range(2)
        ]
        first = (side[0][0] + side[1][1]).astype(BF)
        second = (side[1][0] + side[0][1]).astype(BF)
        for copy in range(out.shape[0]):
            out[copy, 0] = first
            out[copy, 1] = second

    parts = pltpu.with_memory_space_constraint(parts, pltpu.VMEM)
    return pl.pallas_call(
        kernel, out_shape=jax.ShapeDtypeStruct((32, 2) + parts.shape[3:], BF),
        in_specs=[pl.BlockSpec(memory_space=pltpu.VMEM)],
    )(parts)


def finish(me, parts, queries):
    rows, lanes = parts.shape[-2:]
    count, width = queries.shape
    examples = parts.shape[0] * parts.shape[2] * parts.shape[3]
    cuts = 4
    span = width // cuts

    def kernel(me_ref, ref, q_hbm, grads_ref, scores_ref, q_ref, table, sems):
        loads = [
            pltpu.make_async_copy(
                q_hbm.at[:, pl.ds(k * span, span)], q_ref.at[:, pl.ds(k * span, span)], sems.at[k]
            )
            for k in range(cuts)
        ]
        for load in loads:
            load.start()
        for y in range(4):
            for core in range(2):
                for z in range(2):
                    e = z * 8 + y * 2 + core
                    table[e * rows : (e + 1) * rows, :] = sum(
                        ref[y, k, core, z].astype(F32) for k in range(4)
                    )
        total = None
        for cut in range(cuts):
            loads[cut].wait()
            pieces = []
            for k in range(cut * rows // cuts, (cut + 1) * rows // cuts):
                pieces.append(table[pl.ds(k, examples, stride=rows), :].astype(BF))
                grads_ref[:, k * lanes : (k + 1) * lanes] = table[
                    pl.ds(me_ref[0] * rows + k, 1), :
                ]
            term = nt(
                jnp.concatenate(pieces, axis=1), q_ref[:, cut * span : (cut + 1) * span]
            )
            total = term if total is None else total + term
        scores_ref[...] = total

    hbm = pl.BlockSpec(memory_space=pltpu.HBM)
    vmem = pl.BlockSpec(memory_space=pltpu.VMEM)
    parts = pltpu.with_memory_space_constraint(parts, pltpu.VMEM)
    return pl.pallas_call(
        kernel,
        out_shape=(
            jax.ShapeDtypeStruct((1, rows * lanes), F32),
            jax.ShapeDtypeStruct((examples, count), F32),
        ),
        in_specs=[
            pl.BlockSpec(memory_space=pltpu.SMEM),
            vmem,
            hbm,
        ],
        out_specs=(vmem, vmem),
        scratch_shapes=[
            pltpu.VMEM(queries.shape, BF),
            pltpu.VMEM((examples * rows, lanes), F32),
            pltpu.SemaphoreType.DMA((cuts,)),
        ],
    )(me, parts, queries)


def along_y(v, forward):
    pairs = []
    for y in range(4):
        for core in range(2):
            step = 1 if (core == 0) == forward else 3
            pairs.append((2 * y + core, 2 * ((y + step) % 4) + core))
    return lax.ppermute(v, ("y", "c"), pairs)


def trade(copies, axes):
    return lax.all_to_all(copies, axes, 0, 0, tiled=True)


def on_device(inputs, gate_pre, up_out, weight, out_grad, seed_in, seed_out, queries):
    seq, block = out_grad.shape[0], weight.shape[1]
    rank = seed_in.shape[1]
    zh, y, c, zl, x = (lax.axis_index(name).astype(jnp.int32) for name in DP + TP)
    half = seq // 2

    w_one = along_y(weight, True)
    w_two = along_y(weight, False)
    m_own = flip(weight, "c")
    start = ((1 - zh) * 8 + ((y + x) % 4) * 2) * block
    odd = zl % 2
    far_a = lax.dynamic_slice(out_grad, (odd * half, start), (half, 2 * block))
    far_a = flip(far_a, "zh")
    far_b = lax.ppermute(far_a, "zl", [(0, 1), (1, 0), (2, 3), (3, 2)])

    proj = (seed_out.astype(F32) * 0.25 * (2.0 * FF) ** (-0.5)).astype(BF)
    gate = gate_pre.astype(F32)
    sigma = jax.nn.sigmoid(gate)
    act = (up_out.astype(F32) * sigma * (1.0 + gate * (1.0 - sigma))).astype(BF)
    one, two = jnp.where(c == 0, 3, 1), jnp.where(c == 0, 1, 3)
    slabs = [(0, c), (0, 1 - c), (one, c), (two, 1 - c), (two, c), (one, 1 - c), (2, c), (2, 1 - c)]
    index = [zh, x, odd, zh] + [zh * 8 + ((y + j) % 4) * 2 for j in range(4)]
    for j, core in slabs:
        index += [j, core]
    index = jnp.stack([jnp.asarray(v, jnp.int32) for v in index])
    act, proj, index = lax.optimization_barrier((act, proj, index))
    act_far = flip(act, "zh")

    order = jnp.concatenate([jnp.arange(0, rank, 2), jnp.arange(1, rank, 2)])
    pick = (jnp.arange(rank)[:, None] == order[None, :]).astype(BF)
    proj_in = (seed_in.astype(F32) * (2.0 * D) ** (-0.5)).astype(BF)
    proj_in = jnp.dot(proj_in, pick, preferred_element_type=F32).astype(BF)
    left = lax.dot_general(
        proj_in, inputs, (((0,), (1,)), ((), ())), preferred_element_type=F32
    ).astype(BF)
    left = sum(fetch(left, "x", s).astype(F32) for s in (1, 2, 3)) + left.astype(F32)
    left_all = everyone(left.astype(BF), ("zh", "zl"), 8)

    pieces_a = [far_a] + [fetch(far_a, "x", s) for s in (1, 2, 3)]
    pieces_b = [far_b] + [fetch(far_b, "x", s) for s in (1, 2, 3)]

    m_one = flip(w_one, "c")
    m_two = flip(w_two, "c")
    w_opp = along_y(w_one, True)
    m_opp = flip(w_opp, "c")

    mats = (weight, m_own, w_one, m_one, w_two, m_two)
    right, sums, rows = slab_sums(index, out_grad, pieces_a, pieces_b, mats, act, proj)
    right, sums = middle(index, rows, w_opp, right, sums, act, proj)
    payload = project(index, rows, m_opp, right, sums, (act, act_far), proj, left_all)
    z_all = trade(payload, ("zh", "zl"))
    merged = merge(z_all.reshape(2, 4, 2, rank // 2, 2 * rank))
    every = trade(merged, ("y", "x", "c"))
    me = (zh * 8 + y * 2 + c).reshape(1)
    every = every.reshape(4, 4, 2, 2, rank // 2, 2 * rank)
    return finish(me, every, queries)


def solution(mesh):
    fine = Mesh(mesh.devices.reshape(2, 4, 2, 4, 4), DP + TP)
    in_specs = (
        P(DP, TP),
        P(DP, TP),
        P(DP, TP),
        P(TP, DP),
        P(DP, None),
        P(TP, None),
        P(TP, None),
        P(DP + TP, None),
    )
    out_specs = (P(DP, None), P(None, DP + TP))

    return jax.shard_map(
        on_device, mesh=fine, in_specs=in_specs, out_specs=out_specs, check_vma=False
    )
```

```python
import jax
import jax.numpy as jnp
from jax import lax
from jax.experimental import pallas as pl
from jax.experimental.pallas import tpu as pltpu
from jax.sharding import Mesh, PartitionSpec as P


D = 8192
FF = 28672
BF = jnp.bfloat16
F32 = jnp.float32
DP = ("zh", "y", "c")
TP = ("zl", "x")
WIDE = 896
TILE = 256


def flip(v, axis):
    return lax.ppermute(v, axis, [(0, 1), (1, 0)])


def fetch(v, axis, step):
    return lax.ppermute(v, axis, [((i + step) % 4, i) for i in range(4)])


def everyone(v, axes, count):
    copies = jnp.broadcast_to(v[None], (count,) + v.shape)
    return lax.all_to_all(copies, axes, 0, 0, tiled=True)


def nt(rows, weight):
    return lax.dot_general(rows, weight, (((1,), (1,)), ((), ())), preferred_element_type=F32)


def slab_sums(index, near, pieces_a, pieces_b, mats, act, proj):
    n = len(mats)
    seq, ff = act.shape
    block, rank = mats[0].shape[1], proj.shape[1]
    half, pair = seq // 2, 2 * block

    def kernel(s, *refs):
        near_ref, parts_a, parts_b, mat = refs[0], refs[1:5], refs[5:9], refs[9 : 9 + n]
        act_ref, proj_ref, right, out, kept, rows, sems = refs[9 + n :]

        @pl.when(pl.program_id(0) == 0)
        def _():
            copies = []
            for j in range(4):
                at = pl.multiple_of(s[4 + j] * block, block)
                source = near_ref.at[:, pl.ds(at, pair)]
                copies.append((source, rows.at[j, pl.ds(0, seq)]))
            for r in range(4):
                slot = lax.rem(s[1] + r, 4)
                at_a = pl.multiple_of(seq + s[2] * half, half)
                at_b = pl.multiple_of(seq + (1 - s[2]) * half, half)
                copies.append((parts_a[r], rows.at[slot, pl.ds(at_a, half)]))
                copies.append((parts_b[r], rows.at[slot, pl.ds(at_b, half)]))
            copies = [
                pltpu.make_async_copy(source, target, sems.at[k])
                for k, (source, target) in enumerate(copies)
            ]
            for copy in copies:
                copy.start()
            for copy in copies:
                copy.wait()
            kept[...] = rows[2]
            right[...] = jnp.zeros_like(right)

        total = None
        for t in range(n):
            at = pl.multiple_of(s[8 + 2 * t + 1] * block, block)
            term = nt(rows[s[8 + 2 * t], :, pl.ds(at, block)], mat[t][...])
            total = term if total is None else total + term
        out[...] = total[seq:]
        grad = (total[:seq] * act_ref[...].astype(F32)).astype(BF)
        right[...] += jnp.dot(grad, proj_ref[...], preferred_element_type=F32)

    return pl.pallas_call(
        kernel,
        out_shape=(
            jax.ShapeDtypeStruct((seq, rank), F32),
            jax.ShapeDtypeStruct((seq, ff), F32),
            jax.ShapeDtypeStruct((2 * seq, pair), BF),
        ),
        grid_spec=pltpu.PrefetchScalarGridSpec(
            num_scalar_prefetch=1,
            grid=(ff // TILE,),
            in_specs=[pl.BlockSpec(memory_space=pl.ANY)] * 9
            + [pl.BlockSpec((TILE, block), lambda i, s: (i, 0))] * n
            + [
                pl.BlockSpec((seq, TILE), lambda i, s: (0, i)),
                pl.BlockSpec((TILE, rank), lambda i, s: (i, 0)),
            ],
            out_specs=(
                pl.BlockSpec((seq, rank), lambda i, s: (0, 0)),
                pl.BlockSpec((seq, TILE), lambda i, s: (0, i)),
                pl.BlockSpec((2 * seq, pair), lambda i, s: (0, 0)),
            ),
            scratch_shapes=[
                pltpu.VMEM((4, 2 * seq, pair), BF),
                pltpu.SemaphoreType.DMA((12,)),
            ],
        ),
    )(index, near, *pieces_a, *pieces_b, *mats, act, proj)


def middle(index, rows, mat, right, sums, act, proj):
    seq, ff = sums.shape
    block, rank = mat.shape[1], proj.shape[1]

    def kernel(_, rows_ref, mat_ref, right_ref, sum_ref, act_ref, proj_ref, out, sum_out):
        @pl.when(pl.program_id(0) == 0)
        def _():
            out[...] = right_ref[...]

        total = nt(rows_ref[...], mat_ref[...])
        sum_out[...] = sum_ref[...] + total[seq:]
        grad = (total[:seq] * act_ref[...].astype(F32)).astype(BF)
        out[...] += jnp.dot(grad, proj_ref[...], preferred_element_type=F32)

    wide = pl.BlockSpec((seq, WIDE), lambda i, s: (0, i))
    small = pl.BlockSpec((seq, rank), lambda i, s: (0, 0))
    return pl.pallas_call(
        kernel,
        out_shape=(jax.ShapeDtypeStruct((seq, rank), F32), jax.ShapeDtypeStruct((seq, ff), F32)),
        grid_spec=pltpu.PrefetchScalarGridSpec(
            num_scalar_prefetch=1,
            grid=(ff // WIDE,),
            in_specs=[
                pl.BlockSpec((2 * seq, block), lambda i, s: (0, s[21])),
                pl.BlockSpec((WIDE, block), lambda i, s: (i, 0)),
                small,
                wide,
                wide,
                pl.BlockSpec((WIDE, rank), lambda i, s: (i, 0)),
            ],
            out_specs=(small, wide),
        ),
    )(index, rows, mat, right, sums, act, proj)


def project(index, rows, mat, right, sums, acts, proj, left_all):
    seq, ff = sums.shape
    block, rank = mat.shape[1], proj.shape[1]
    half = rank // 2
    steps = ff // WIDE

    def kernel(s, rows_hbm, mat_hbm, right_hbm, sum_hbm, near_hbm, far_hbm, proj_hbm, left_hbm,
               out, rows_ref, mat_ref, right_n, sum_ref, act_n, act_f, proj_ref, left_ref, sems):
        at = pl.multiple_of(s[23] * block, block)
        moves = [(rows_hbm.at[:, pl.ds(at, block)], rows_ref)]
        waits = []
        for k in range(steps):
            span = pl.ds(k * WIDE, WIDE)
            waits.append(len(moves))
            moves += [
                (mat_hbm.at[span], mat_ref.at[span]),
                (near_hbm.at[:, span], act_n.at[:, span]),
                (proj_hbm.at[span], proj_ref.at[span]),
                (sum_hbm.at[:, span], sum_ref.at[:, span]),
                (far_hbm.at[:, span], act_f.at[:, span]),
            ]
            if k == 0:
                moves.append((right_hbm, right_n))
        waits.append(len(moves))
        moves.append((left_hbm, left_ref))
        copies = [
            pltpu.make_async_copy(source, target, sems.at[k])
            for k, (source, target) in enumerate(moves)
        ]
        for copy in copies:
            copy.start()
        copies[0].wait()
        sides = [None, None]
        for k in range(steps):
            for copy in copies[waits[k] : waits[k + 1]]:
                copy.wait()
            span = slice(k * WIDE, (k + 1) * WIDE)
            total = nt(rows_ref[...], mat_ref[span, :])
            hiddens = (total[:seq], sum_ref[:, span] + total[seq:])
            for i, (hidden, act) in enumerate(zip(hiddens, (act_n, act_f))):
                grad = (hidden * act[:, span].astype(F32)).astype(BF)
                term = jnp.dot(grad, proj_ref[span, :], preferred_element_type=F32)
                sides[i] = term if sides[i] is None else sides[i] + term
        sides[0] = sides[0] + right_n[...]
        copies[-1].wait()
        pieces = []
        for z, side in ((s[0], sides[0]), (1 - s[0], sides[1])):
            left = sum(left_ref[4 * z + k].astype(F32) for k in range(4)).astype(BF)
            outer = jnp.dot(left, side.astype(BF), preferred_element_type=F32)
            pieces.append(jnp.concatenate([outer[:half], outer[half:]], axis=1).astype(BF))
        for copy in range(out.shape[0]):
            out[copy, :half, :] = pieces[0]
            out[copy, half:, :] = pieces[1]

    hbm = pl.BlockSpec(memory_space=pltpu.HBM)
    return pl.pallas_call(
        kernel,
        out_shape=jax.ShapeDtypeStruct((8, rank, 2 * rank), BF),
        in_specs=[pl.BlockSpec(memory_space=pltpu.SMEM)] + [hbm] * 8,
        out_specs=pl.BlockSpec(memory_space=pltpu.VMEM),
        scratch_shapes=[
            pltpu.VMEM((2 * seq, block), BF),
            pltpu.VMEM(mat.shape, BF),
            pltpu.VMEM(right.shape, F32),
            pltpu.VMEM(sums.shape, F32),
            pltpu.VMEM(sums.shape, BF),
            pltpu.VMEM(sums.shape, BF),
            pltpu.VMEM(proj.shape, BF),
            pltpu.VMEM(left_all.shape, BF),
            pltpu.SemaphoreType.DMA((3 + 5 * steps,)),
        ],
    )(index, rows, mat, right, sums, *acts, proj, left_all)


def merge(parts):
    def kernel(ref, out):
        side = [
            [sum(ref[z, k, g].astype(F32) for k in range(4)) for g in range(2)] for z in range(2)
        ]
        first = (side[0][0] + side[1][1]).astype(BF)
        second = (side[1][0] + side[0][1]).astype(BF)
        for copy in range(out.shape[0]):
            out[copy, 0] = first
            out[copy, 1] = second

    parts = pltpu.with_memory_space_constraint(parts, pltpu.VMEM)
    return pl.pallas_call(
        kernel, out_shape=jax.ShapeDtypeStruct((32, 2) + parts.shape[3:], BF),
        in_specs=[pl.BlockSpec(memory_space=pltpu.VMEM)],
    )(parts)


def finish(me, parts, queries):
    rows, lanes = parts.shape[-2:]
    count, width = queries.shape
    examples = parts.shape[0] * parts.shape[2] * parts.shape[3]
    cuts = 4
    span = width // cuts

    def kernel(me_ref, ref, q_hbm, grads_ref, scores_ref, q_ref, table, sems):
        loads = [
            pltpu.make_async_copy(
                q_hbm.at[:, pl.ds(k * span, span)], q_ref.at[:, pl.ds(k * span, span)], sems.at[k]
            )
            for k in range(cuts)
        ]
        for load in loads:
            load.start()
        for y in range(4):
            for core in range(2):
                for z in range(2):
                    e = z * 8 + y * 2 + core
                    table[e * rows : (e + 1) * rows, :] = sum(
                        ref[y, k, core, z].astype(F32) for k in range(4)
                    )
        total = None
        for cut in range(cuts):
            loads[cut].wait()
            pieces = []
            for k in range(cut * rows // cuts, (cut + 1) * rows // cuts):
                pieces.append(table[pl.ds(k, examples, stride=rows), :].astype(BF))
                grads_ref[:, k * lanes : (k + 1) * lanes] = table[
                    pl.ds(me_ref[0] * rows + k, 1), :
                ]
            term = nt(
                jnp.concatenate(pieces, axis=1), q_ref[:, cut * span : (cut + 1) * span]
            )
            total = term if total is None else total + term
        scores_ref[...] = total

    hbm = pl.BlockSpec(memory_space=pltpu.HBM)
    vmem = pl.BlockSpec(memory_space=pltpu.VMEM)
    parts = pltpu.with_memory_space_constraint(parts, pltpu.VMEM)
    return pl.pallas_call(
        kernel,
        out_shape=(
            jax.ShapeDtypeStruct((1, rows * lanes), F32),
            jax.ShapeDtypeStruct((examples, count), F32),
        ),
        in_specs=[
            pl.BlockSpec(memory_space=pltpu.SMEM),
            vmem,
            hbm,
        ],
        out_specs=(vmem, vmem),
        scratch_shapes=[
            pltpu.VMEM(queries.shape, BF),
            pltpu.VMEM((examples * rows, lanes), F32),
            pltpu.SemaphoreType.DMA((cuts,)),
        ],
    )(me, parts, queries)


def along_y(v, forward):
    pairs = []
    for y in range(4):
        for core in range(2):
            step = 1 if (core == 0) == forward else 3
            pairs.append((2 * y + core, 2 * ((y + step) % 4) + core))
    return lax.ppermute(v, ("y", "c"), pairs)


def trade(copies, axes):
    return lax.all_to_all(copies, axes, 0, 0, tiled=True)


def on_device(inputs, gate_pre, up_out, weight, out_grad, seed_in, seed_out, queries):
    seq, block = out_grad.shape[0], weight.shape[1]
    rank = seed_in.shape[1]
    zh, y, c, zl, x = (lax.axis_index(name).astype(jnp.int32) for name in DP + TP)
    half = seq // 2

    w_one = along_y(weight, True)
    w_two = along_y(weight, False)
    m_own = flip(weight, "c")
    start = ((1 - zh) * 8 + ((y + x) % 4) * 2) * block
    odd = zl % 2
    far_a = lax.dynamic_slice(out_grad, (odd * half, start), (half, 2 * block))
    far_a = flip(far_a, "zh")
    far_b = lax.ppermute(far_a, "zl", [(0, 1), (1, 0), (2, 3), (3, 2)])

    proj = (seed_out.astype(F32) * 0.25 * (2.0 * FF) ** (-0.5)).astype(BF)
    gate = gate_pre.astype(F32)
    sigma = jax.nn.sigmoid(gate)
    act = (up_out.astype(F32) * sigma * (1.0 + gate * (1.0 - sigma))).astype(BF)
    one, two = jnp.where(c == 0, 3, 1), jnp.where(c == 0, 1, 3)
    slabs = [(0, c), (0, 1 - c), (one, c), (two, 1 - c), (two, c), (one, 1 - c), (2, c), (2, 1 - c)]
    index = [zh, x, odd, zh] + [zh * 8 + ((y + j) % 4) * 2 for j in range(4)]
    for j, core in slabs:
        index += [j, core]
    index = jnp.stack([jnp.asarray(v, jnp.int32) for v in index])
    act, proj, index = lax.optimization_barrier((act, proj, index))
    act_far = flip(act, "zh")

    order = jnp.concatenate([jnp.arange(0, rank, 2), jnp.arange(1, rank, 2)])
    pick = (jnp.arange(rank)[:, None] == order[None, :]).astype(BF)
    proj_in = (seed_in.astype(F32) * (2.0 * D) ** (-0.5)).astype(BF)
    proj_in = jnp.dot(proj_in, pick, preferred_element_type=F32).astype(BF)
    left = lax.dot_general(
        proj_in, inputs, (((0,), (1,)), ((), ())), preferred_element_type=F32
    ).astype(BF)
    left = sum(fetch(left, "x", s).astype(F32) for s in (1, 2, 3)) + left.astype(F32)
    left_all = everyone(left.astype(BF), ("zh", "zl"), 8)

    pieces_a = [far_a] + [fetch(far_a, "x", s) for s in (1, 2, 3)]
    pieces_b = [far_b] + [fetch(far_b, "x", s) for s in (1, 2, 3)]

    m_one = flip(w_one, "c")
    m_two = flip(w_two, "c")
    w_opp = along_y(w_one, True)
    m_opp = flip(w_opp, "c")

    mats = (weight, m_own, w_one, m_one, w_two, m_two)
    right, sums, rows = slab_sums(index, out_grad, pieces_a, pieces_b, mats, act, proj)
    right, sums = middle(index, rows, w_opp, right, sums, act, proj)
    payload = project(index, rows, m_opp, right, sums, (act, act_far), proj, left_all)
    z_all = trade(payload, ("zh", "zl"))
    merged = merge(z_all.reshape(2, 4, 2, rank // 2, 2 * rank))
    every = trade(merged, ("y", "x", "c"))
    me = (zh * 8 + y * 2 + c).reshape(1)
    every = every.reshape(4, 4, 2, 2, rank // 2, 2 * rank)
    return finish(me, every, queries)


def solution(mesh):
    fine = Mesh(mesh.devices.reshape(2, 4, 2, 4, 4), DP + TP)
    in_specs = (
        P(DP, TP),
        P(DP, TP),
        P(DP, TP),
        P(TP, DP),
        P(DP, None),
        P(TP, None),
        P(TP, None),
        P(DP + TP, None),
    )
    out_specs = (P(DP, None), P(None, DP + TP))

    return jax.shard_map(
        on_device, mesh=fine, in_specs=in_specs, out_specs=out_specs, check_vma=False
    )
```
